32 devices in a mesh: groups: 2 (over y), row: 16 (over z, x, core).
Axes of the slice: x: 2, y: 2, z: 4, core: 2. Of those that a mesh axis runs over, the one named last changes fastest.
Arguments:
- activations: bfloat16 [768, 8192], P('groups', 'row'), parts along dimension 0, may hold values from -24 to 24
- norm_gain: bfloat16 [8192], P('row'), may hold values from 0.099609375 to 1.8984375
- gate_weight: bfloat16 [8192, 28672], P(None, 'row'), may hold values from -0.0625 to 0.0625
- up_weight: bfloat16 [8192, 28672], P(None, 'row'), may hold values from -0.0625 to 0.0625
- down_weight: bfloat16 [28672, 8192], P('row'), may hold values from -0.046875 to 0.046875
Outputs:
- mlp_out: bfloat16 [768, 8192], P('groups', 'row'), parts along dimension 0
The draws below stay inside these ranges and needn't reach their ends.
There are 2 independent parts, one for each index of `groups`. The reference program is written for one: setup_inputs(seed, part) draws one part's arguments, and reference() takes and returns one part's arrays. A program takes and returns all parts, laid end to end along the dimension named above; an argument that names none is the same for every part. Nothing has to cross between parts.
All inputs are finite; a program needn't handle non-finite values.
Results may differ from the reference program's by a relative error of at most 0.0065.
Values may be sent and summed in bfloat16 or wider, within the bound.
A program may use at most 192 MiB of HBM per device.

```python
import jax
import jax.numpy as jnp
from jax import lax

D = 8192
FF = 28672
TOKENS = 384


def draw_activations(key, part):
    key_cols, key_rows, key_base = jax.random.split(key, 3)
    position = jnp.arange(D, dtype=jnp.float32) / max(D - 1, 1)
    column_scale = jnp.exp(jax.random.uniform(key_cols, (D,), jnp.float32) * jnp.log(10.0))
    row_scale = jnp.exp(jax.random.uniform(key_rows, (TOKENS, 1), jnp.float32) * jnp.log(10.0))
    rising = 3.0 ** position
    base_values = jax.random.truncated_normal(key_base, -4.0, 4.0, (TOKENS, D), jnp.float32)
    result = jnp.clip(base_values * row_scale * (column_scale * rising)[None, :] * 0.05, -24.0, 24.0)
    return result.astype(jnp.bfloat16)


def strengthened(values, rng, source, target, shards_of, factor):
    owner, partner = [(jnp.arange(values.shape[dim]) // (values.shape[dim] // shards_of)).reshape([-1 if axis == dim else 1 for axis in range(values.ndim)]) for dim in (source, target)]
    chosen = jax.random.permutation(rng, shards_of)[partner]
    strong = (owner == chosen) | (owner == (partner + shards_of // 2) % shards_of)
    return jnp.where(strong, factor * values, values)


def block_scale(rng, shape, pieces, low, top_value):
    def one(dim, parts):
        heights = jax.random.uniform(jax.random.fold_in(jax.random.fold_in(rng, 6), dim), (parts,), jnp.float32, low / len(pieces), top_value / len(pieces))
        return jnp.repeat(jnp.exp(heights), shape[dim] // parts).reshape((-1,) + (1,) * (len(shape) - dim - 1))

    gain = one(*pieces[0])
    for cut in pieces[1:]:
        gain = gain * one(*cut)
    return gain


def bell_draw(key, extent, spread, limit, shards=(), kind=jnp.bfloat16):
    values = jax.random.normal(key, extent, jnp.float32) * spread
    if len(shards) > 0:
        values = block_scale(key, extent, shards, -0.22, 0.18) * values
    return jnp.clip(values, min=-limit, max=limit).astype(kind)


def gaussian_with(own_key, extent, scale, reach, cuts, heavy, held_as=jnp.bfloat16):
    values = scale * jax.random.normal(own_key, extent, jnp.float32)
    if cuts:
        values = values * block_scale(own_key, extent, cuts, -0.22, 0.18)
    return jnp.clip(strengthened(values, jax.random.fold_in(own_key, 3), *heavy), -reach, reach).astype(held_as)


def setup_inputs(seed: int = 0, part: int = 0) -> dict:
    arg_keys = jax.random.split(jax.random.key(seed), 6)
    own_keys = jax.random.split(jax.random.fold_in(arg_keys[5], part), 6)
    activations = draw_activations(jax.random.fold_in(jax.random.fold_in(arg_keys[5], part), 71), part)
    norm_gain = jnp.clip(1.0 + 0.18 * jax.random.normal(arg_keys[1], (D,), jnp.float32), 0.099609375, 1.8984375).astype(jnp.bfloat16)
    gate_weight = bell_draw(arg_keys[2], (D, FF), D ** -0.5, 0.0625, ((1, 16),))
    up_weight = bell_draw(arg_keys[3], (D, FF), D ** -0.5, 0.0625, ((1, 16),))
    down_weight = gaussian_with(arg_keys[4], (FF, D), FF ** -0.5, 0.046875, ((0, 16),), (0, 1, 16, 2.0))
    return {"activations": activations, "norm_gain": norm_gain, "gate_weight": gate_weight, "up_weight": up_weight, "down_weight": down_weight}


def reference(activations, norm_gain, gate_weight, up_weight, down_weight):
    float_rows = activations.astype(jnp.float32)
    mean_square = lax.optimization_barrier(jnp.mean(float_rows * float_rows, axis=1, keepdims=True))
    normed = (float_rows * lax.rsqrt(mean_square + 1e-05) * norm_gain.astype(jnp.float32)[None, :]).astype(jnp.bfloat16)
    gate_proj = jnp.dot(normed, gate_weight, preferred_element_type=jnp.float32)
    up_proj = jnp.dot(normed, up_weight, preferred_element_type=jnp.float32)
    hidden = (jax.nn.silu(gate_proj) * up_proj).astype(jnp.bfloat16)
    return jnp.dot(hidden, down_weight, preferred_element_type=jnp.float32).astype(jnp.bfloat16)
```

```python
import functools

import jax
import jax.numpy as jnp
from jax import lax
from jax.experimental import pallas as pl
from jax.experimental.pallas import tpu as pltpu
from jax.sharding import PartitionSpec as P

D = 8192
Z, X, H = 4, 2, 2
COLS = 256
MESH = pl.DeviceIdType.MESH
NEAR = ((0, 1, 2, 3), (1, 0, 2, 3), (2, 1, 3, 0), (3, 2, 1, 0))
ORDER_END = (0, 1, 4, 2, 5, 3, 6, 7)
ORDER_MID = (0, 1, 2, 4, 3, 5, 6, 7)


def plain(activations, norm_gain, gate_weight, up_weight, down_weight):
    float_rows = activations.astype(jnp.float32)
    square_sums = lax.psum(jnp.sum(float_rows * float_rows, axis=1), "row")
    inv_scale = lax.rsqrt(square_sums / D + 1e-05)
    normed = (float_rows * inv_scale[:, None] * norm_gain.astype(jnp.float32)[None, :]).astype(
        jnp.bfloat16
    )
    shard_rows = lax.all_gather(normed, "row", axis=1, tiled=True)
    gate_proj = jnp.dot(shard_rows, gate_weight, preferred_element_type=jnp.float32)
    up_proj = jnp.dot(shard_rows, up_weight, preferred_element_type=jnp.float32)
    hidden = (jax.nn.silu(gate_proj) * up_proj).astype(jnp.bfloat16)
    reduced = lax.psum_scatter(
        lax.dot_general(
            down_weight, hidden, (((0,), (1,)), ((), ())), preferred_element_type=jnp.float32
        ),
        "row",
        scatter_dimension=0,
        tiled=True,
    )
    return reduced.T.astype(jnp.bfloat16)


def pick(table, index):
    value = jnp.int32(table[0])
    for at in range(1, len(table)):
        value = jnp.where(index == at, jnp.int32(table[at]), value)
    return value


def near_z(z, k):
    value = pick(NEAR[0], k)
    for at in range(1, Z):
        value = jnp.where(z == at, pick(NEAR[at], k), value)
    return value


def kernel(
    act, gain, gate_w, up_w, down_w, out,
    gathered, stats, squares, inv, xn, w_buf, acc, hidden, dw_buf,
    core_out, core_in, x_out, x_in, z_out, z_in, total,
    act_sem, w_sem, dw_sem, stat_send, stat_recv,
    g_recv, g_up, g_down, g_x, g_core,
    core_send, core_recv, x_send, x_recv, z_send, z_recv,
):
    n = 2 * Z * X
    me = lax.axis_index("row")
    c = lax.rem(me, 2)
    x = lax.rem(me // 2, X)
    z = me // (2 * X)
    tokens, wide = hidden.shape
    half = tokens // H
    feat = gathered.shape[3]
    steps = Z * X
    partner = me + 1 - 2 * c
    across = me + 2 - 4 * x
    above = jnp.minimum(me + 2 * X, n - 1)
    below = jnp.maximum(me - 2 * X, 0)

    def remote(src, dst, send, recv, target):
        return pltpu.make_async_remote_copy(
            src_ref=src, dst_ref=dst, send_sem=send, recv_sem=recv,
            device_id={"row": target}, device_id_type=MESH,
        )

    def place(s):
        code = jnp.where(
            (z == 0) | (z == Z - 1), pick(ORDER_END, s), pick(ORDER_MID, s)
        )
        in_line = code < Z
        k = lax.rem(code, Z)
        zz = near_z(z, k)
        chip = zz * X + jnp.where(in_line, x, 1 - x)
        return in_line, k, zz, chip

    def weights(s):
        _, _, _, chip = place(s)
        rows = pl.ds(pl.multiple_of(chip * 2 * feat, 2 * feat), 2 * feat)
        slot = lax.rem(s, 2)
        return [
            pltpu.make_async_copy(w.at[rows], w_buf.at[slot, i], w_sem.at[slot, i])
            for i, w in enumerate((gate_w, up_w))
        ]

    def dest(kk):
        k = Z - 1 - lax.rem(kk, Z)
        zz = near_z(z, k)
        return zz, zz * X + jnp.where(kk < Z, 1 - x, x)

    def down(kk, mine):
        _, chip = dest(kk)
        core = jnp.where(mine == 1, c, 1 - c)
        cols = pl.ds(pl.multiple_of((chip * 2 + core) * feat, feat), feat)
        slot = lax.rem(kk, 2) * 2 + mine
        return pltpu.make_async_copy(down_w.at[:, cols], dw_buf.at[slot], dw_sem.at[slot])

    own = pltpu.make_async_copy(act, gathered.at[me], act_sem)
    own.start()
    for copy in weights(0) + weights(1):
        copy.start()

    barrier = pltpu.get_barrier_semaphore()
    for step in range(1, n):
        pl.semaphore_signal(
            barrier, inc=1, device_id={"row": lax.rem(me + step, n)}, device_id_type=MESH
        )

    own.wait()
    for h in range(H):
        rows = gathered[me, h].astype(jnp.float32)
        sums = jnp.sum(rows * rows, axis=1, keepdims=True)
        squares[h * half : (h + 1) * half, :] = jnp.broadcast_to(sums, (half, 128))
    blocks = tokens // 128
    lines = feat // 128
    for b in range(blocks):
        stats[me, b : b + 1, :] = squares[b * 128 : (b + 1) * 128, :].T[0:1, :]
    for j in range(lines):
        stats[me, blocks + j : blocks + j + 1, :] = gain[:, j * 128 : (j + 1) * 128].astype(
            jnp.float32
        )
    pl.semaphore_wait(barrier, n - 1)

    def stat_copy(step):
        return remote(
            stats.at[me], stats.at[me], stat_send.at[step - 1], stat_recv.at[me],
            lax.rem(me + step, n),
        )

    for step in range(1, n):
        stat_copy(step).start()

    def onward(s, h):
        in_line, k, zz, chip = place(s)
        chunk = chip * 2 + c
        ref, recv = gathered.at[chunk, h], g_recv.at[chunk, h]
        return (
            (remote(ref, ref, g_x.at[k, h], recv, across), in_line),
            (remote(ref, ref, g_up.at[k, h], recv, above), in_line & (zz <= z) & (z < Z - 1)),
            (remote(ref, ref, g_down.at[k, h], recv, below), in_line & (zz >= z) & (z > 0)),
            (remote(ref, ref, g_core.at[s, h], recv, partner), s >= 0),
        )

    def arrived(chunk, h):
        ref = gathered.at[chunk, h]
        pltpu.make_async_copy(ref, ref, g_recv.at[chunk, h]).wait()

    def pass_on(s, h):
        for copy, needed in onward(s, h):
            @pl.when(needed)
            def _():
                copy.start()

    for h in range(H):
        pass_on(jnp.int32(0), h)
    acc[...] = jnp.zeros_like(acc)
    for kk in range(2):
        for mine in range(2):
            down(jnp.int32(kk), mine).start()

    for step in range(1, n):
        origin = lax.rem(me + step, n)
        pltpu.make_async_copy(stats.at[origin], stats.at[origin], stat_recv.at[origin]).wait()
    sums = stats[0]
    for origin in range(1, n):
        sums = sums + stats[origin]
    scale = lax.rsqrt(sums / (n * feat) + 1e-05)
    for b in range(blocks):
        inv[b * 128 : (b + 1) * 128, :] = jnp.broadcast_to(scale[b : b + 1, :], (128, 128)).T

    def gather_step(s, carry):
        _, _, _, chip = place(s)
        slot = lax.rem(s, 2)
        for h in range(H):
            arrived(chip * 2 + 1 - c, h)
        for core in range(2):
            for h in range(H):
                rows = slice(h * half, (h + 1) * half)
                for j in range(lines):
                    part = gathered[chip * 2 + core, h, :, j * 128 : (j + 1) * 128]
                    scaled = part.astype(jnp.float32) * inv[rows, :]
                    scaled = scaled * stats[chip * 2 + core, blocks + j : blocks + j + 1, :]
                    at = core * feat + j * 128
                    xn[rows, at : at + 128] = scaled.astype(jnp.bfloat16)
        for i in range(2):
            weights(s)[i].wait()
            acc[i] += jnp.dot(xn[...], w_buf[slot, i], preferred_element_type=jnp.float32)

            @pl.when(s < steps - 2)
            def _():
                weights(s + 2)[i].start()

            @pl.when(s < steps - 1)
            def _():
                _, _, _, chip_next = place(s + 1)
                arrived(chip_next * 2 + c, i)
                pass_on(s + 1, i)

        return carry

    lax.fori_loop(0, steps, gather_step, 0)

    def activate(t, carry):
        cols = pl.ds(pl.multiple_of(t * COLS, COLS), COLS)
        gate = acc[0, :, cols]
        hidden[:, cols] = (gate / (1.0 + jnp.exp(-gate)) * acc[1, :, cols]).astype(jnp.bfloat16)
        return carry

    lax.fori_loop(0, wide // COLS, activate, 0)

    def core_copy(kk):
        return remote(
            core_out.at[kk], core_in.at[kk], core_send.at[kk], core_recv.at[kk], partner
        )

    def x_copy(k, h):
        return remote(x_out.at[k, h], x_in.at[k, h], x_send.at[k, h], x_recv.at[k, h], across)

    def z_copy(zz, h, side, target):
        return remote(
            z_out.at[zz, h], z_in.at[side, zz, h], z_send.at[zz, h], z_recv.at[side, zz, h], target
        )

    def reduce_step(kk, carry):
        zz, _ = dest(kk)
        k = lax.rem(kk, Z)
        for mine in range(2):
            down(kk, mine).wait()
            slot = lax.rem(kk, 2) * 2 + mine
            part = jnp.dot(hidden[...], dw_buf[slot], preferred_element_type=jnp.float32)
            if mine:
                total[...] = part
            else:
                core_out[kk] = part.astype(jnp.bfloat16)
                core_copy(kk).start()

            @pl.when(kk < steps - 2)
            def _():
                down(kk + 2, mine).start()

        core_copy(kk).wait_recv()

        @pl.when(kk < Z)
        def _():
            for h in range(H):
                rows = slice(h * half, (h + 1) * half)
                joined = total[rows, :] + core_in[kk, rows, :].astype(jnp.float32)
                x_out[k, h] = joined.astype(jnp.bfloat16)
                x_copy(k, h).start()

        @pl.when(kk >= Z)
        def _():
            for h in range(H):
                rows = slice(h * half, (h + 1) * half)
                joined = total[rows, :] + core_in[kk, rows, :].astype(jnp.float32)
                x_copy(k, h).wait_recv()
                total[rows, :] = joined + x_in[k, h].astype(jnp.float32)

                @pl.when((z > 0) & (zz >= z))
                def _():
                    z_copy(zz, h, 0, above).wait_recv()
                    total[rows, :] += z_in[0, zz, h].astype(jnp.float32)

                @pl.when((z < Z - 1) & (zz <= z))
                def _():
                    z_copy(zz, h, 1, below).wait_recv()
                    total[rows, :] += z_in[1, zz, h].astype(jnp.float32)

                @pl.when(zz == z)
                def _():
                    out[rows, :] = total[rows, :].astype(jnp.bfloat16)

                @pl.when(zz != z)
                def _():
                    z_out[zz, h] = total[rows, :].astype(jnp.bfloat16)

                @pl.when(zz > z)
                def _():
                    z_copy(zz, h, 0, above).start()

                @pl.when(zz < z)
                def _():
                    z_copy(zz, h, 1, below).start()

        return carry

    lax.fori_loop(0, steps, reduce_step, 0)

    for step in range(1, n):
        stat_copy(step).wait_send()

    def drain(s, carry):
        for h in range(H):
            for copy, needed in onward(s, h):
                @pl.when(needed)
                def _():
                    copy.wait_send()
        core_copy(s).wait_send()
        return carry

    lax.fori_loop(0, steps, drain, 0)

    def drain_sums(k, carry):
        for h in range(H):
            x_copy(k, h).wait_send()

            @pl.when(k != z)
            def _():
                z_copy(k, h, 0, above).wait_send()
        return carry

    lax.fori_loop(0, Z, drain_sums, 0)


def fused(activations, norm_gain, gate_weight, up_weight, down_weight):
    tokens, feat = activations.shape
    wide = gate_weight.shape[1]
    n, steps, half = 2 * Z * X, Z * X, tokens // H
    bf16, f32 = jnp.bfloat16, jnp.float32
    anywhere = pl.BlockSpec(memory_space=pl.ANY)
    vmem = pl.BlockSpec(memory_space=pltpu.VMEM)
    dma = pltpu.SemaphoreType.DMA
    return pl.pallas_call(
        kernel,
        out_shape=jax.ShapeDtypeStruct((tokens, feat), bf16),
        in_specs=[anywhere, vmem, anywhere, anywhere, anywhere],
        out_specs=vmem,
        scratch_shapes=[
            pltpu.VMEM((n, H, half, feat), bf16),
            pltpu.VMEM((n, 8, 128), f32),
            pltpu.VMEM((tokens, 128), f32),
            pltpu.VMEM((tokens, 128), f32),
            pltpu.VMEM((tokens, 2 * feat), bf16),
            pltpu.VMEM((2, 2, 2 * feat, wide), bf16),
            pltpu.VMEM((2, tokens, wide), f32),
            pltpu.VMEM((tokens, wide), bf16),
            pltpu.VMEM((4, wide, feat), bf16),
            pltpu.VMEM((steps, tokens, feat), bf16),
            pltpu.VMEM((steps, tokens, feat), bf16),
            pltpu.VMEM((Z, H, half, feat), bf16),
            pltpu.VMEM((Z, H, half, feat), bf16),
            pltpu.VMEM((Z, H, half, feat), bf16),
            pltpu.VMEM((2, Z, H, half, feat), bf16),
            pltpu.VMEM((tokens, feat), f32),
            dma,
            dma((2, 2)),
            dma((4,)),
            dma((n - 1,)),
            dma((n,)),
            dma((n, H)),
            dma((Z, H)),
            dma((Z, H)),
            dma((Z, H)),
            dma((steps, H)),
            dma((steps,)),
            dma((steps,)),
            dma((Z, H)),
            dma((Z, H)),
            dma((Z, H)),
            dma((2, Z, H)),
        ],
        compiler_params=pltpu.CompilerParams(
            collective_id=0, has_side_effects=True, vmem_limit_bytes=62 * 2**20
        ),
    )(
        activations.reshape(H, half, feat), norm_gain.reshape(1, feat),
        gate_weight, up_weight, down_weight,
    )


def solution(mesh):
    in_specs = (P("groups", "row"), P("row"), P(None, "row"), P(None, "row"), P("row", None))
    out_specs = P("groups", "row")
    n = mesh.shape["row"]

    def per_device(activations, norm_gain, gate_weight, up_weight, down_weight):
        tokens, feat = activations.shape
        fits = (
            n == 2 * Z * X
            and tokens % 128 == 0
            and tokens % (16 * H) == 0
            and tokens // 128 + feat // 128 <= 8
            and feat % 128 == 0
            and gate_weight.shape[1] % COLS == 0
        )
        body = fused if fits else plain
        return body(activations, norm_gain, gate_weight, up_weight, down_weight)

    return jax.shard_map(
        per_device, mesh=mesh, in_specs=in_specs, out_specs=out_specs, check_vma=False
    )
```

```python
import functools

import jax
import jax.numpy as jnp
from jax import lax
from jax.experimental import pallas as pl
from jax.experimental.pallas import tpu as pltpu
from jax.sharding import PartitionSpec as P

D = 8192
Z, X, H = 4, 2, 2
COLS = 256
MESH = pl.DeviceIdType.MESH
NEAR = ((0, 1, 2, 3), (1, 0, 2, 3), (2, 1, 3, 0), (3, 2, 1, 0))
ORDER_END = (0, 1, 4, 2, 5, 3, 6, 7)
ORDER_MID = (0, 1, 2, 4, 3, 5, 6, 7)


def plain(activations, norm_gain, gate_weight, up_weight, down_weight):
    float_rows = activations.astype(jnp.float32)
    square_sums = lax.psum(jnp.sum(float_rows * float_rows, axis=1), "row")
    inv_scale = lax.rsqrt(square_sums / D + 1e-05)
    normed = (float_rows * inv_scale[:, None] * norm_gain.astype(jnp.float32)[None, :]).astype(
        jnp.bfloat16
    )
    shard_rows = lax.all_gather(normed, "row", axis=1, tiled=True)
    gate_proj = jnp.dot(shard_rows, gate_weight, preferred_element_type=jnp.float32)
    up_proj = jnp.dot(shard_rows, up_weight, preferred_element_type=jnp.float32)
    hidden = (jax.nn.silu(gate_proj) * up_proj).astype(jnp.bfloat16)
    reduced = lax.psum_scatter(
        lax.dot_general(
            down_weight, hidden, (((0,), (1,)), ((), ())), preferred_element_type=jnp.float32
        ),
        "row",
        scatter_dimension=0,
        tiled=True,
    )
    return reduced.T.astype(jnp.bfloat16)


def pick(table, index):
    value = jnp.int32(table[0])
    for at in range(1, len(table)):
        value = jnp.where(index == at, jnp.int32(table[at]), value)
    return value


def near_z(z, k):
    value = pick(NEAR[0], k)
    for at in range(1, Z):
        value = jnp.where(z == at, pick(NEAR[at], k), value)
    return value


def kernel(
    act, gain, gate_w, up_w, down_w, out,
    gathered, stats, squares, inv, xn, w_buf, acc, hidden, dw_buf,
    core_out, core_in, x_out, x_in, z_out, z_in, total,
    act_sem, w_sem, dw_sem, stat_send, stat_recv,
    g_recv, g_up, g_down, g_x, g_core,
    core_send, core_recv, x_send, x_recv, z_send, z_recv,
):
    n = 2 * Z * X
    me = lax.axis_index("row")
    c = lax.rem(me, 2)
    x = lax.rem(me // 2, X)
    z = me // (2 * X)
    tokens, wide = hidden.shape
    half = tokens // H
    feat = gathered.shape[3]
    steps = Z * X
    partner = me + 1 - 2 * c
    across = me + 2 - 4 * x
    above = jnp.minimum(me + 2 * X, n - 1)
    below = jnp.maximum(me - 2 * X, 0)

    def remote(src, dst, send, recv, target):
        return pltpu.make_async_remote_copy(
            src_ref=src, dst_ref=dst, send_sem=send, recv_sem=recv,
            device_id={"row": target}, device_id_type=MESH,
        )

    def place(s):
        code = jnp.where(
            (z == 0) | (z == Z - 1), pick(ORDER_END, s), pick(ORDER_MID, s)
        )
        in_line = code < Z
        k = lax.rem(code, Z)
        zz = near_z(z, k)
        chip = zz * X + jnp.where(in_line, x, 1 - x)
        return in_line, k, zz, chip

    def weights(s):
        _, _, _, chip = place(s)
        rows = pl.ds(pl.multiple_of(chip * 2 * feat, 2 * feat), 2 * feat)
        slot = lax.rem(s, 2)
        return [
            pltpu.make_async_copy(w.at[rows], w_buf.at[slot, i], w_sem.at[slot, i])
            for i, w in enumerate((gate_w, up_w))
        ]

    def dest(kk):
        k = Z - 1 - lax.rem(kk, Z)
        zz = near_z(z, k)
        return zz, zz * X + jnp.where(kk < Z, 1 - x, x)

    def down(kk, mine):
        _, chip = dest(kk)
        core = jnp.where(mine == 1, c, 1 - c)
        cols = pl.ds(pl.multiple_of((chip * 2 + core) * feat, feat), feat)
        slot = lax.rem(kk, 2) * 2 + mine
        return pltpu.make_async_copy(down_w.at[:, cols], dw_buf.at[slot], dw_sem.at[slot])

    own = pltpu.make_async_copy(act, gathered.at[me], act_sem)
    own.start()
    for copy in weights(0) + weights(1):
        copy.start()

    barrier = pltpu.get_barrier_semaphore()
    for step in range(1, n):
        pl.semaphore_signal(
            barrier, inc=1, device_id={"row": lax.rem(me + step, n)}, device_id_type=MESH
        )

    own.wait()
    for h in range(H):
        rows = gathered[me, h].astype(jnp.float32)
        sums = jnp.sum(rows * rows, axis=1, keepdims=True)
        squares[h * half : (h + 1) * half, :] = jnp.broadcast_to(sums, (half, 128))
    blocks = tokens // 128
    lines = feat // 128
    for b in range(blocks):
        stats[me, b : b + 1, :] = squares[b * 128 : (b + 1) * 128, :].T[0:1, :]
    for j in range(lines):
        stats[me, blocks + j : blocks + j + 1, :] = gain[:, j * 128 : (j + 1) * 128].astype(
            jnp.float32
        )
    pl.semaphore_wait(barrier, n - 1)

    def stat_copy(step):
        return remote(
            stats.at[me], stats.at[me], stat_send.at[step - 1], stat_recv.at[me],
            lax.rem(me + step, n),
        )

    for step in range(1, n):
        stat_copy(step).start()

    def onward(s, h):
        in_line, k, zz, chip = place(s)
        chunk = chip * 2 + c
        ref, recv = gathered.at[chunk, h], g_recv.at[chunk, h]
        return (
            (remote(ref, ref, g_x.at[k, h], recv, across), in_line),
            (remote(ref, ref, g_up.at[k, h], recv, above), in_line & (zz <= z) & (z < Z - 1)),
            (remote(ref, ref, g_down.at[k, h], recv, below), in_line & (zz >= z) & (z > 0)),
            (remote(ref, ref, g_core.at[s, h], recv, partner), s >= 0),
        )

    def arrived(chunk, h):
        ref = gathered.at[chunk, h]
        pltpu.make_async_copy(ref, ref, g_recv.at[chunk, h]).wait()

    def pass_on(s, h):
        for copy, needed in onward(s, h):
            @pl.when(needed)
            def _():
                copy.start()

    for h in range(H):
        pass_on(jnp.int32(0), h)
    acc[...] = jnp.zeros_like(acc)
    for kk in range(2):
        for mine in range(2):
            down(jnp.int32(kk), mine).start()

    for step in range(1, n):
        origin = lax.rem(me + step, n)
        pltpu.make_async_copy(stats.at[origin], stats.at[origin], stat_recv.at[origin]).wait()
    sums = stats[0]
    for origin in range(1, n):
        sums = sums + stats[origin]
    scale = lax.rsqrt(sums / (n * feat) + 1e-05)
    for b in range(blocks):
        inv[b * 128 : (b + 1) * 128, :] = jnp.broadcast_to(scale[b : b + 1, :], (128, 128)).T

    def gather_step(s, carry):
        _, _, _, chip = place(s)
        slot = lax.rem(s, 2)
        for h in range(H):
            arrived(chip * 2 + 1 - c, h)
        for core in range(2):
            for h in range(H):
                rows = slice(h * half, (h + 1) * half)
                for j in range(lines):
                    part = gathered[chip * 2 + core, h, :, j * 128 : (j + 1) * 128]
                    scaled = part.astype(jnp.float32) * inv[rows, :]
                    scaled = scaled * stats[chip * 2 + core, blocks + j : blocks + j + 1, :]
                    at = core * feat + j * 128
                    xn[rows, at : at + 128] = scaled.astype(jnp.bfloat16)
        for i in range(2):
            @pl.when(s < steps - 1)
            def _():
                _, _, _, chip_next = place(s + 1)
                for h in range(i * H // 2, (i + 1) * H // 2):
                    arrived(chip_next * 2 + c, h)
                    pass_on(s + 1, h)

            weights(s)[i].wait()
            acc[i] += jnp.dot(xn[...], w_buf[slot, i], preferred_element_type=jnp.float32)

            @pl.when(s < steps - 2)
            def _():
                weights(s + 2)[i].start()

        return carry

    lax.fori_loop(0, steps, gather_step, 0)

    def activate(t, carry):
        cols = pl.ds(pl.multiple_of(t * COLS, COLS), COLS)
        gate = acc[0, :, cols]
        hidden[:, cols] = (gate / (1.0 + jnp.exp(-gate)) * acc[1, :, cols]).astype(jnp.bfloat16)
        return carry

    lax.fori_loop(0, wide // COLS, activate, 0)

    def core_copy(kk):
        return remote(
            core_out.at[kk], core_in.at[kk], core_send.at[kk], core_recv.at[kk], partner
        )

    def x_copy(k, h):
        return remote(x_out.at[k, h], x_in.at[k, h], x_send.at[k, h], x_recv.at[k, h], across)

    def z_copy(zz, h, side, target):
        return remote(
            z_out.at[zz, h], z_in.at[side, zz, h], z_send.at[zz, h], z_recv.at[side, zz, h], target
        )

    def reduce_step(kk, carry):
        zz, _ = dest(kk)
        k = lax.rem(kk, Z)
        for mine in range(2):
            down(kk, mine).wait()
            slot = lax.rem(kk, 2) * 2 + mine
            part = jnp.dot(hidden[...], dw_buf[slot], preferred_element_type=jnp.float32)
            if mine:
                total[...] = part
            else:
                core_out[kk] = part.astype(jnp.bfloat16)
                core_copy(kk).start()

            @pl.when(kk < steps - 2)
            def _():
                down(kk + 2, mine).start()

        core_copy(kk).wait_recv()

        @pl.when(kk < Z)
        def _():
            for h in range(H):
                rows = slice(h * half, (h + 1) * half)
                joined = total[rows, :] + core_in[kk, rows, :].astype(jnp.float32)
                x_out[k, h] = joined.astype(jnp.bfloat16)
                x_copy(k, h).start()

        @pl.when(kk >= Z)
        def _():
            for h in range(H):
                rows = slice(h * half, (h + 1) * half)
                joined = total[rows, :] + core_in[kk, rows, :].astype(jnp.float32)
                x_copy(k, h).wait_recv()
                total[rows, :] = joined + x_in[k, h].astype(jnp.float32)

                @pl.when((z > 0) & (zz >= z))
                def _():
                    z_copy(zz, h, 0, above).wait_recv()
                    total[rows, :] += z_in[0, zz, h].astype(jnp.float32)

                @pl.when((z < Z - 1) & (zz <= z))
                def _():
                    z_copy(zz, h, 1, below).wait_recv()
                    total[rows, :] += z_in[1, zz, h].astype(jnp.float32)

                @pl.when(zz == z)
                def _():
                    out[rows, :] = total[rows, :].astype(jnp.bfloat16)

                @pl.when(zz != z)
                def _():
                    z_out[zz, h] = total[rows, :].astype(jnp.bfloat16)

                @pl.when(zz > z)
                def _():
                    z_copy(zz, h, 0, above).start()

                @pl.when(zz < z)
                def _():
                    z_copy(zz, h, 1, below).start()

        return carry

    lax.fori_loop(0, steps, reduce_step, 0)

    for step in range(1, n):
        stat_copy(step).wait_send()

    def drain(s, carry):
        for h in range(H):
            for copy, needed in onward(s, h):
                @pl.when(needed)
                def _():
                    copy.wait_send()
        core_copy(s).wait_send()
        return carry

    lax.fori_loop(0, steps, drain, 0)

    def drain_sums(k, carry):
        for h in range(H):
            x_copy(k, h).wait_send()

            @pl.when(k != z)
            def _():
                z_copy(k, h, 0, above).wait_send()
        return carry

    lax.fori_loop(0, Z, drain_sums, 0)


def fused(activations, norm_gain, gate_weight, up_weight, down_weight):
    tokens, feat = activations.shape
    wide = gate_weight.shape[1]
    n, steps, half = 2 * Z * X, Z * X, tokens // H
    bf16, f32 = jnp.bfloat16, jnp.float32
    anywhere = pl.BlockSpec(memory_space=pl.ANY)
    vmem = pl.BlockSpec(memory_space=pltpu.VMEM)
    dma = pltpu.SemaphoreType.DMA
    return pl.pallas_call(
        kernel,
        out_shape=jax.ShapeDtypeStruct((tokens, feat), bf16),
        in_specs=[anywhere, vmem, anywhere, anywhere, anywhere],
        out_specs=vmem,
        scratch_shapes=[
            pltpu.VMEM((n, H, half, feat), bf16),
            pltpu.VMEM((n, 8, 128), f32),
            pltpu.VMEM((tokens, 128), f32),
            pltpu.VMEM((tokens, 128), f32),
            pltpu.VMEM((tokens, 2 * feat), bf16),
            pltpu.VMEM((2, 2, 2 * feat, wide), bf16),
            pltpu.VMEM((2, tokens, wide), f32),
            pltpu.VMEM((tokens, wide), bf16),
            pltpu.VMEM((4, wide, feat), bf16),
            pltpu.VMEM((steps, tokens, feat), bf16),
            pltpu.VMEM((steps, tokens, feat), bf16),
            pltpu.VMEM((Z, H, half, feat), bf16),
            pltpu.VMEM((Z, H, half, feat), bf16),
            pltpu.VMEM((Z, H, half, feat), bf16),
            pltpu.VMEM((2, Z, H, half, feat), bf16),
            pltpu.VMEM((tokens, feat), f32),
            dma,
            dma((2, 2)),
            dma((4,)),
            dma((n - 1,)),
            dma((n,)),
            dma((n, H)),
            dma((Z, H)),
            dma((Z, H)),
            dma((Z, H)),
            dma((steps, H)),
            dma((steps,)),
            dma((steps,)),
            dma((Z, H)),
            dma((Z, H)),
            dma((Z, H)),
            dma((2, Z, H)),
        ],
        compiler_params=pltpu.CompilerParams(
            collective_id=0, has_side_effects=True, vmem_limit_bytes=62 * 2**20
        ),
    )(
        activations.reshape(H, half, feat), norm_gain.reshape(1, feat),
        gate_weight, up_weight, down_weight,
    )


def solution(mesh):
    in_specs = (P("groups", "row"), P("row"), P(None, "row"), P(None, "row"), P("row", None))
    out_specs = P("groups", "row")
    n = mesh.shape["row"]

    def per_device(activations, norm_gain, gate_weight, up_weight, down_weight):
        tokens, feat = activations.shape
        fits = (
            n == 2 * Z * X
            and tokens % 128 == 0
            and tokens % (16 * H) == 0
            and tokens // 128 + feat // 128 <= 8
            and feat % 128 == 0
            and gate_weight.shape[1] % COLS == 0
        )
        body = fused if fits else plain
        return body(activations, norm_gain, gate_weight, up_weight, down_weight)

    return jax.shard_map(
        per_device, mesh=mesh, in_specs=in_specs, out_specs=out_specs, check_vma=False
    )
```
